128 devices in a mesh: lsec: 8 (over y, core), rsec: 16 (over x, z).
Axes of the slice: x: 4, y: 4, z: 4, core: 2. Of those that a mesh axis runs over, the one named last changes fastest.
Arguments:
- two_site: bfloat16 [2, 32, 128, 8192], P(None, 'lsec', None, 'rsec'), may hold values from -6 to 6
- left_env: bfloat16 [34, 32, 128, 128], P(None, 'lsec', 'rsec'), may hold values from -0.09375 to 0.09375
- right_env: bfloat16 [34, 64, 128, 128], P(None, 'rsec', 'lsec'), may hold values from -0.5 to 0.5
- left_size: int32 [32], P('lsec'), may hold values from 16 to 128, as said below
- right_size: int32 [64], P('rsec'), may hold values from 16 to 128, as said below
- channel_shift: int32 [34, 2], replicated, may hold values from -2 to 2, as said below
Outputs:
- applied: bfloat16 [2, 32, 128, 8192], P(None, 'lsec', None, 'rsec')
The draws below stay inside these ranges and needn't reach their ends.
Inputs may be any that keep to these rules, and one draw needn't show every extreme that they name: `left_size`: each sector holds 16 to 128 states; some left sector and some right sector hold exactly 128. `right_size`: as for left_size. `channel_shift`: every offset from -2 to 2 is the left offset of some channel and the right offset of some channel.
All inputs are finite; a program needn't handle non-finite values.
Results may differ from the reference program's by a relative error of at most 0.0049.
Values may be sent and summed in bfloat16 or wider, within the bound.
No kernel may reach another device: no remote copies, remote signals or barrier semaphores. Data moves between devices by JAX's collectives and lax.ppermute only.
A program may use at most 64 MiB of HBM per device.

```python
import jax
import jax.numpy as jnp
from jax import lax

SB = 128
KCH = 34
VECS = 2
SHIFT = 2
NL = 32
NR = 64
DL = 4096
DR = 8192


def sector_sizes(key, count):
    sizes = jax.random.randint(key, (count,), SB // 8, SB + 1)
    spot = jax.random.randint(jax.random.fold_in(key, 7), (), 0, count)
    return sizes.at[spot].set(SB).astype(jnp.int32)


def draw_left_size(key, part):
    return sector_sizes(jax.random.fold_in(key, 11), NL)


def draw_right_size(key, part):
    return sector_sizes(jax.random.fold_in(key, 13), NR)


def draw_channel_shift(key, part):
    spread = 2 * SHIFT + 1
    left_part = jax.random.permutation(jax.random.fold_in(key, 1), KCH) % spread - SHIFT
    right_part = jax.random.permutation(jax.random.fold_in(key, 2), KCH) % spread - SHIFT
    return jnp.stack([left_part, right_part], axis=1).astype(jnp.int32)


def block_levels(key, extent, split, smallest, largest):
    factor_of, own = 1.0, jax.random.fold_in(key, 6)
    for axis_at, shards_of in split:
        draws = jnp.exp(jax.random.uniform(jax.random.fold_in(own, axis_at), (shards_of,), jnp.float32, smallest / len(split), largest / len(split)))
        factor_of = factor_of * jnp.repeat(draws, extent[axis_at] // shards_of).reshape([-1 if axis == axis_at else 1 for axis in range(len(extent))])
    return factor_of


def bell_draw(rng, extent, scale, bound, pieces=(), held_as=jnp.bfloat16):
    drawn = scale * jax.random.normal(rng, extent, jnp.float32)
    if pieces:
        drawn = drawn * block_levels(rng, extent, pieces, -0.22, 0.18)
    return jnp.clip(drawn, -bound, bound).astype(held_as)


def setup_inputs(seed: int = 0) -> dict:
    streams_of = jax.random.split(jax.random.key(seed), 7)
    two_site = bell_draw(streams_of[0], (VECS, NL, SB, DR), 1.0, 6.0, ((1, 8), (3, 16)))
    left_env = bell_draw(streams_of[1], (KCH, NL, SB, SB), (SB * KCH) ** -0.5, 0.09375, ((1, 8), (2, 16)))
    right_env = bell_draw(streams_of[2], (KCH, NR, SB, SB), SB ** -0.5, 0.5, ((1, 16), (2, 8)))
    left_size = draw_left_size(jax.random.fold_in(streams_of[6], 71), 0)
    right_size = draw_right_size(jax.random.fold_in(streams_of[6], 71), 0)
    channel_shift = draw_channel_shift(jax.random.fold_in(streams_of[6], 71), 0)
    return {"two_site": two_site, "left_env": left_env, "right_env": right_env, "left_size": left_size, "right_size": right_size, "channel_shift": channel_shift}


def live_states(sizes, count):
    states = jnp.arange(SB, dtype=jnp.int32)
    return (states[None, :] < sizes[:, None]).astype(jnp.float32).reshape(count * SB)


def reference(two_site, left_env, right_env, left_size, right_size, channel_shift):
    row_live = live_states(left_size, NL)
    col_live = live_states(right_size, NR)
    weights = row_live[:, None] * col_live[None, :]
    masked = (two_site.astype(jnp.float32).reshape(VECS, DL, DR) * weights[None]).reshape(VECS, NL, SB, NR, SB)
    padded = jnp.pad(masked, ((0, 0), (SHIFT, SHIFT), (0, 0), (SHIFT, SHIFT), (0, 0)))
    left_expanded = left_env.astype(jnp.float32)
    right_wide = right_env.astype(jnp.float32)

    def one_channel(operator_bond_index, cumulative_sum):
        left_sector_offset = (SHIFT - channel_shift[operator_bond_index, 0]).astype(jnp.int32)
        right_start = (SHIFT - channel_shift[operator_bond_index, 1]).astype(jnp.int32)
        zero_index = jnp.int32(0)
        source = lax.dynamic_slice(padded, (zero_index, left_sector_offset, zero_index, right_start, zero_index), (VECS, NL, SB, NR, SB))
        right_reduced = jnp.einsum("vlarb,rcb->vlarc", source, right_wide[operator_bond_index]).astype(jnp.bfloat16)
        right_reduced = lax.optimization_barrier(right_reduced).astype(jnp.float32)
        return cumulative_sum + jnp.einsum("jit,xjtum->xjium", left_expanded[operator_bond_index], right_reduced)

    cumulative_sum = lax.fori_loop(0, KCH, one_channel, jnp.zeros((VECS, NL, SB, NR, SB), jnp.float32))
    result = cumulative_sum.reshape(VECS, DL, DR) * weights[None]
    return result.astype(jnp.bfloat16).reshape(VECS, NL, SB, DR)
```

```python
import functools

import jax
import jax.numpy as jnp
from jax import lax
from jax.experimental import pallas as pl
from jax.experimental.pallas import tpu as pltpu
from jax.sharding import PartitionSpec as P

KCH = 34
SHIFT = 2
SPLIT = 18
XN, ZN, YN, CORES = 4, 4, 4, 2
NT = (((1,), (1,)), ((), ()))
NN = (((1,), (0,)), ((), ()))


def shifted_x(step):
    return [(ZN * x + z, ZN * ((x + step) % XN) + z) for x in range(XN) for z in range(ZN)]


def shifted_z(step):
    return [(ZN * x + z, ZN * x + (z + step) % ZN) for x in range(XN) for z in range(ZN)]


def shifted_y(step):
    return [(CORES * y + c, CORES * ((y + step) % YN) + c) for y in range(YN) for c in range(CORES)]


def ring_of_four(value, axis, shifted):
    half = value.shape[0] // 2
    left = lax.ppermute(value, axis, shifted(1))
    right = lax.ppermute(value, axis, shifted(-1))
    far_a = lax.ppermute(left[:half], axis, shifted(1))
    far_b = lax.ppermute(right[half:], axis, shifted(-1))
    return left, right, far_a, far_b


def four_segments(count):
    half = count // 2
    return (
        (0, 0, count, 0),
        (count, 0, count, -1),
        (2 * count, 0, count, 1),
        (3 * count, 0, half, 2),
        (3 * count + half, half, half, 2),
    )


def bundle_segments(count):
    inner = four_segments(count)
    rows = 4 * count
    half = rows // 2
    found = []
    for row, start, many, step in inner:
        found.append((0, row, start, many, step, 0))
        found.append((1, row, start, many, step, -1))
        found.append((2, row, start, many, step, 1))
        if row < half:
            found.append((3, row, start, many, step, 2))
        else:
            found.append((4, row - half, start, many, step, 2))
    return tuple(found)


def live_states(sizes, padded_extent):
    states = jnp.arange(padded_extent, dtype=jnp.int32)
    return states[None, :] < sizes[:, None]


def channels_kernel(
    first, count, z_first, is_first, is_last,
    shift, left_size, right_size,
    own, low_l, high_l, low_r, high_r, lefts, rights, *rest,
):
    rest = list(rest)
    total_in = None if is_first else rest.pop(0)
    out = rest.pop(0)
    source, left_all, right_all = rest[:3]
    rest = rest[3:]
    if is_last:
        total = rest.pop(0)
    else:
        total = out
    sems = rest.pop(0)
    rsec, lsec = lax.axis_index("rsec"), lax.axis_index("lsec")
    x, z, y, core = rsec // ZN, lax.rem(rsec, ZN), lsec // CORES, lax.rem(lsec, CORES)

    copies = []

    def start(src, dst, which):
        copy = pltpu.make_async_copy(src, dst, sems.at[which])
        copy.start()
        copies.append(copy)

    start(own, source.at[2:6, 2:6], 0)
    start(low_l, source.at[2:6, 0:2], 1)
    start(high_l, source.at[2:6, 6:8], 2)
    start(low_r, source.at[0:2], 3)
    start(high_r, source.at[6:8], 4)
    at = 5
    for row, begin, many, step in four_segments(KCH):
        lo, hi = max(begin, first), min(begin + many, first + count)
        if hi <= lo:
            continue
        for which, side in ((0, core), (1, 1 - core)):
            rows = 16 * (CORES * lax.rem(y + step + YN, YN) + side)
            start(
                rights[which].at[row + lo - begin : row + hi - begin],
                right_all.at[lo - first : hi - first, :, pl.ds(pl.multiple_of(rows, 16), 16)],
                at,
            )
            at += 1
    for which, row, begin, many, inner, outer in bundle_segments(count):
        dx, dz = (outer, inner) if z_first else (inner, outer)
        rows = 8 * (ZN * lax.rem(x + dx + XN, XN) + lax.rem(z + dz + ZN, ZN))
        start(
            lefts[which].at[row : row + many],
            left_all.at[begin : begin + many, :, pl.ds(pl.multiple_of(rows, 8), 8)],
            at,
        )
        at += 1
    if is_first:
        total[...] = jnp.zeros_like(total)
    else:
        start(total_in, total, at)
    for copy in copies:
        copy.wait()

    def two_channels(pair, carry):
        ks = (2 * pair, 2 * pair + 1)
        shifts = [(shift[first + k, 0], shift[first + k, 1]) for k in ks]
        for r in range(4):
            partial = []
            for k, (dl, dr) in zip(ks, shifts):
                rows = source[r + SHIFT - dr, pl.ds(SHIFT - dl, 4)].reshape(4 * 256, 128)
                partial.append(
                    lax.dot_general(
                        rows, right_all[k, r], NT, preferred_element_type=jnp.float32
                    ).astype(jnp.bfloat16)
                )
            for l in range(4):
                stacked = jnp.concatenate(
                    [
                        jnp.concatenate(
                            [p[l * 256 : l * 256 + 128], p[l * 256 + 128 : l * 256 + 256]], axis=1
                        )
                        for p in partial
                    ],
                    axis=0,
                )
                sides = jnp.concatenate([left_all[k, l] for k in ks], axis=1)
                total[l, r] += lax.dot_general(
                    sides, stacked, NN, preferred_element_type=jnp.float32
                )
        return carry

    lax.fori_loop(0, count // 2, two_channels, 0)

    if is_last:
        row = lax.broadcasted_iota(jnp.int32, (128, 128), 0)
        col = lax.broadcasted_iota(jnp.int32, (128, 128), 1)
        for l in range(4):
            for r in range(4):
                live = (row < left_size[l]) & (col < right_size[r])
                for v in range(2):
                    block = total[l, r, :, v * 128 : v * 128 + 128]
                    out[v, l, :, r * 128 : r * 128 + 128] = jnp.where(live, block, 0.0).astype(
                        jnp.bfloat16
                    )


def run_channels(first, count, z_first, is_first, is_last, scalars, sources, lefts, rights, total):
    totals = jax.ShapeDtypeStruct((4, 4, 128, 256), jnp.float32)
    result = jax.ShapeDtypeStruct((2, 4, 128, 512), jnp.bfloat16)
    anywhere = pl.BlockSpec(memory_space=pl.ANY)
    smem = pl.BlockSpec(memory_space=pltpu.SMEM)
    operands = [*scalars, *sources, tuple(lefts), tuple(rights)]
    specs = [smem] * 3 + [anywhere] * 5 + [(anywhere,) * len(lefts), (anywhere,) * len(rights)]
    if not is_first:
        operands.append(total)
        specs.append(anywhere)
    scratch = [
        pltpu.VMEM((8, 8, 256, 128), jnp.bfloat16),
        pltpu.VMEM((count, 4, 128, 128), jnp.bfloat16),
        pltpu.VMEM((count, 4, 128, 128), jnp.bfloat16),
    ]
    if is_last:
        scratch.append(pltpu.VMEM((4, 4, 128, 256), jnp.float32))
    scratch.append(pltpu.SemaphoreType.DMA((64,)))
    return pl.pallas_call(
        functools.partial(channels_kernel, first, count, z_first, is_first, is_last),
        out_shape=result if is_last else totals,
        in_specs=specs,
        out_specs=pl.BlockSpec(memory_space=pltpu.VMEM),
        scratch_shapes=scratch,
        compiler_params=pltpu.CompilerParams(vmem_limit_bytes=32 << 20),
        cost_estimate=pl.CostEstimate(
            flops=count * 4 * 4 * 2 * 2 * 2 * 128**3, bytes_accessed=10 << 20, transcendentals=0
        ),
    )(*operands)


def local(two_site, left_env, right_env, left_size, right_size, channel_shift):
    row_live = live_states(left_size, 128)
    col_live = live_states(right_size, 128)
    blocks = two_site.reshape(2, 4, 128, 4, 128)
    live = row_live[None, :, :, None, None] & col_live[None, None, None, :, :]
    own = jnp.where(live, blocks, jnp.bfloat16(0)).transpose(3, 1, 0, 2, 4).reshape(4, 4, 256, 128)

    l_up = [(i, i + 1) for i in range(7)]
    l_down = [(i + 1, i) for i in range(7)]
    r_up = [(i, i + 1) for i in range(15)]
    r_down = [(i + 1, i) for i in range(15)]
    low_l = lax.ppermute(own[:, 2:], "lsec", l_up)
    high_l = lax.ppermute(own[:, :2], "lsec", l_down)
    low_r = lax.ppermute(
        jnp.concatenate([low_l[2:], own[2:], high_l[2:]], axis=1), "rsec", r_up
    )
    high_r = lax.ppermute(
        jnp.concatenate([low_l[:2], own[:2], high_l[:2]], axis=1), "rsec", r_down
    )

    y_bundle = jnp.concatenate([right_env, *ring_of_four(right_env, "lsec", shifted_y)], axis=0)
    partner = lax.ppermute(y_bundle, "lsec", [(i, i ^ 1) for i in range(8)])

    chunk_a = left_env[:SPLIT]
    chunk_b = left_env[SPLIT:]
    z_bundle = jnp.concatenate([chunk_a, *ring_of_four(chunk_a, "rsec", shifted_z)], axis=0)
    x_bundle = jnp.concatenate([chunk_b, *ring_of_four(chunk_b, "rsec", shifted_x)], axis=0)
    lefts_a = (z_bundle, *ring_of_four(z_bundle, "rsec", shifted_x))
    lefts_b = (x_bundle, *ring_of_four(x_bundle, "rsec", shifted_z))

    scalars = (channel_shift, left_size, right_size)
    sources = (own, low_l, high_l, low_r, high_r)
    rights = (y_bundle, partner)
    total = run_channels(0, SPLIT, True, True, False, scalars, sources, lefts_a, rights, None)
    return run_channels(
        SPLIT, KCH - SPLIT, False, False, True, scalars, sources, lefts_b, rights, total
    )


def solution(mesh):
    placed = (
        P(None, "lsec", None, "rsec"),
        P(None, "lsec", "rsec", None),
        P(None, "rsec", "lsec", None),
        P("lsec"),
        P("rsec"),
        P(),
    )
    return jax.shard_map(
        local, mesh=mesh, in_specs=placed, out_specs=P(None, "lsec", None, "rsec"), check_vma=False
    )
```

```python
import functools

import jax
import jax.numpy as jnp
from jax import lax
from jax.experimental import pallas as pl
from jax.experimental.pallas import tpu as pltpu
from jax.sharding import PartitionSpec as P

KCH = 34
SHIFT = 2
SPLIT = 16
XN, ZN, YN, CORES = 4, 4, 4, 2
NT = (((1,), (1,)), ((), ()))
NN = (((1,), (0,)), ((), ()))


def shifted_x(step):
    return [(ZN * x + z, ZN * ((x + step) % XN) + z) for x in range(XN) for z in range(ZN)]


def shifted_z(step):
    return [(ZN * x + z, ZN * x + (z + step) % ZN) for x in range(XN) for z in range(ZN)]


def shifted_y(step):
    return [(CORES * y + c, CORES * ((y + step) % YN) + c) for y in range(YN) for c in range(CORES)]


def mask_kernel(left_size, right_size, two_site, down, up):
    row = lax.broadcasted_iota(jnp.int32, (128, 128), 0)
    col = lax.broadcasted_iota(jnp.int32, (128, 128), 1)
    for l in range(4):
        for r in range(4):
            live = (row < left_size[l]) & (col < right_size[r])
            target = down if r < 2 else up
            for v in range(2):
                block = two_site[v, l, :, r * 128 : r * 128 + 128].astype(jnp.float32)
                target[r % 2, l, v * 128 : v * 128 + 128] = jnp.where(live, block, 0.0).astype(
                    jnp.bfloat16
                )


def masked_halves(two_site, left_size, right_size):
    half = jax.ShapeDtypeStruct((2, 4, 256, 128), jnp.bfloat16)
    smem = pl.BlockSpec(memory_space=pltpu.SMEM)
    vmem = pl.BlockSpec(memory_space=pltpu.VMEM)
    return pl.pallas_call(
        mask_kernel,
        out_shape=(half, half),
        in_specs=[smem, smem, vmem],
        out_specs=(vmem, vmem),
        compiler_params=pltpu.CompilerParams(vmem_limit_bytes=8 << 20),
        cost_estimate=pl.CostEstimate(flops=1 << 20, bytes_accessed=2 << 20, transcendentals=0),
    )(left_size, right_size, two_site)


def rim_kernel(low_r, down, up, high_r, to_next, to_previous):
    for at, part in enumerate((low_r, down, up, high_r)):
        to_next[2 * at : 2 * at + 2] = part[:, 2:4]
        to_previous[2 * at : 2 * at + 2] = part[:, 0:2]


def left_rims(low_r, down, up, high_r):
    rim = jax.ShapeDtypeStruct((8, 2, 256, 128), jnp.bfloat16)
    vmem = pl.BlockSpec(memory_space=pltpu.VMEM)
    return pl.pallas_call(
        rim_kernel,
        out_shape=(rim, rim),
        in_specs=[vmem] * 4,
        out_specs=(vmem, vmem),
        compiler_params=pltpu.CompilerParams(vmem_limit_bytes=12 << 20),
        cost_estimate=pl.CostEstimate(flops=1 << 20, bytes_accessed=4 << 20, transcendentals=0),
    )(low_r, down, up, high_r)


def bundle_kernel(own, left, right, far, first, second):
    for at, part in enumerate((own, left, right, far)):
        first[at] = part[:SPLIT]
        second[at] = part[SPLIT:]


def bundled(own, left, right, far):
    vmem = pl.BlockSpec(memory_space=pltpu.VMEM)
    return pl.pallas_call(
        bundle_kernel,
        out_shape=tuple(
            jax.ShapeDtypeStruct((4, many, 4, 8, 128), jnp.bfloat16)
            for many in (SPLIT, KCH - SPLIT)
        ),
        in_specs=[vmem] * 4,
        out_specs=(vmem, vmem),
        compiler_params=pltpu.CompilerParams(vmem_limit_bytes=8 << 20),
        cost_estimate=pl.CostEstimate(flops=1 << 20, bytes_accessed=2 << 20, transcendentals=0),
    )(own, left, right, far)


RING_STEPS = (0, -1, 1, 2)


def channels_kernel(
    first, count, is_first, is_last, shift, left_size, right_size,
    low_r, down, up, high_r, low_l, high_l, lefts, rights, partners, *rest,
):
    rest = list(rest)
    total_in = None if is_first else rest.pop(0)
    out = rest.pop(0)
    source, left_all, right_all = rest[:3]
    rest = rest[3:]
    total = rest.pop(0) if is_last else out
    sems = rest.pop(0)
    rsec, lsec = lax.axis_index("rsec"), lax.axis_index("lsec")
    x, z, y, core = rsec // ZN, lax.rem(rsec, ZN), lsec // CORES, lax.rem(lsec, CORES)

    copies = []

    def start(src, dst):
        copy = pltpu.make_async_copy(src, dst, sems.at[len(copies)])
        copy.start()
        copies.append(copy)

    for at, part in enumerate((low_r, down, up, high_r)):
        start(part, source.at[2 * at : 2 * at + 2, 2:6])
    start(low_l, source.at[:, 0:2])
    start(high_l, source.at[:, 6:8])
    for step, own, other in zip(RING_STEPS, rights, partners):
        for part, side in ((own, core), (other, 1 - core)):
            row = pl.multiple_of(16 * (CORES * lax.rem(y + step + YN, YN) + side), 16)
            start(part.at[first : first + count], right_all.at[:, :, pl.ds(row, 16)])
    for dx, bundle in zip(RING_STEPS, lefts):
        for at, dz in enumerate(RING_STEPS):
            row = 8 * (ZN * lax.rem(x + dx + XN, XN) + lax.rem(z + dz + ZN, ZN))
            start(bundle.at[at], left_all.at[:, :, pl.ds(pl.multiple_of(row, 8), 8)])
    if is_first:
        total[...] = jnp.zeros_like(total)
    else:
        start(total_in, total)
    for copy in copies:
        copy.wait()

    def two_channels(pair, carry):
        ks = (2 * pair, 2 * pair + 1)
        shifts = [(shift[first + k, 0], shift[first + k, 1]) for k in ks]
        for r in range(4):
            partial = []
            for k, (dl, dr) in zip(ks, shifts):
                rows = source[r + SHIFT - dr, pl.ds(SHIFT - dl, 4)].reshape(4 * 256, 128)
                partial.append(
                    lax.dot_general(
                        rows, right_all[k, r], NT, preferred_element_type=jnp.float32
                    ).astype(jnp.bfloat16)
                )
            for l in range(4):
                stacked = jnp.concatenate(
                    [
                        jnp.concatenate(
                            [p[l * 256 : l * 256 + 128], p[l * 256 + 128 : l * 256 + 256]], axis=1
                        )
                        for p in partial
                    ],
                    axis=0,
                )
                sides = jnp.concatenate([left_all[k, l] for k in ks], axis=1)
                total[l, r] += lax.dot_general(
                    sides, stacked, NN, preferred_element_type=jnp.float32
                )
        return carry

    lax.fori_loop(0, count // 2, two_channels, 0)

    if is_last:
        row = lax.broadcasted_iota(jnp.int32, (128, 128), 0)
        col = lax.broadcasted_iota(jnp.int32, (128, 128), 1)
        for l in range(4):
            for r in range(4):
                live = (row < left_size[l]) & (col < right_size[r])
                for v in range(2):
                    block = total[l, r, :, v * 128 : v * 128 + 128]
                    out[v, l, :, r * 128 : r * 128 + 128] = jnp.where(live, block, 0.0).astype(
                        jnp.bfloat16
                    )


def run_channels(first, count, is_first, is_last, scalars, sources, lefts, rights, partners, total):
    totals = jax.ShapeDtypeStruct((4, 4, 128, 256), jnp.float32)
    result = jax.ShapeDtypeStruct((2, 4, 128, 512), jnp.bfloat16)
    anywhere = pl.BlockSpec(memory_space=pltpu.HBM)
    smem = pl.BlockSpec(memory_space=pltpu.SMEM)
    operands = [*scalars, *sources, tuple(lefts), tuple(rights), tuple(partners)]
    specs = [smem] * 3 + [anywhere] * 6 + [(anywhere,) * 4] * 3
    if not is_first:
        operands.append(total)
        specs.append(anywhere)
    scratch = [
        pltpu.VMEM((8, 8, 256, 128), jnp.bfloat16),
        pltpu.VMEM((count, 4, 128, 128), jnp.bfloat16),
        pltpu.VMEM((count, 4, 128, 128), jnp.bfloat16),
    ]
    if is_last:
        scratch.append(pltpu.VMEM((4, 4, 128, 256), jnp.float32))
    scratch.append(pltpu.SemaphoreType.DMA((40,)))
    return pl.pallas_call(
        functools.partial(channels_kernel, first, count, is_first, is_last),
        out_shape=result if is_last else totals,
        in_specs=specs,
        out_specs=pl.BlockSpec(memory_space=pltpu.VMEM),
        scratch_shapes=scratch,
        compiler_params=pltpu.CompilerParams(vmem_limit_bytes=60 * 1024 * 1024),
        cost_estimate=pl.CostEstimate(
            flops=count * 4 * 4 * 2 * 2 * 2 * 128**3, bytes_accessed=10 << 20, transcendentals=0
        ),
    )(*operands)


def local(two_site, left_env, right_env, left_size, right_size, channel_shift):
    down, up = masked_halves(two_site, left_size, right_size)
    l_up = [(i, i + 1) for i in range(7)]
    l_down = [(i + 1, i) for i in range(7)]
    r_up = [(i, i + 1) for i in range(15)]
    r_down = [(i + 1, i) for i in range(15)]
    low_r = lax.ppermute(up, "rsec", r_up)
    high_r = lax.ppermute(down, "rsec", r_down)
    to_next, to_previous = left_rims(low_r, down, up, high_r)
    low_l = lax.ppermute(to_next, "lsec", l_up)
    high_l = lax.ppermute(to_previous, "lsec", l_down)

    z_ring = [lax.ppermute(left_env, "rsec", shifted_z(step)) for step in (1, -1, 2)]
    rights = [right_env] + [lax.ppermute(right_env, "lsec", shifted_y(s)) for s in (1, -1, 2)]
    swap = [(i, i ^ 1) for i in range(8)]
    partners = [lax.ppermute(part, "lsec", swap) for part in rights]

    bundle_a, bundle_b = bundled(left_env, *z_ring)
    left_a = lax.ppermute(bundle_a, "rsec", shifted_x(1))
    right_a = lax.ppermute(bundle_a, "rsec", shifted_x(-1))
    far_a = lax.ppermute(left_a, "rsec", shifted_x(1))
    left_b = lax.ppermute(bundle_b, "rsec", shifted_x(1))
    right_b = lax.ppermute(bundle_b, "rsec", shifted_x(-1))
    far_b = lax.ppermute(right_b, "rsec", shifted_x(-1))

    scalars = (channel_shift, left_size, right_size)
    sources = (low_r, down, up, high_r, low_l, high_l)
    lefts_a = (bundle_a, left_a, right_a, far_a)
    lefts_b = (bundle_b, left_b, right_b, far_b)
    total = run_channels(
        0, SPLIT, True, False, scalars, sources, lefts_a, rights, partners, None
    )
    return run_channels(
        SPLIT, KCH - SPLIT, False, True, scalars, sources, lefts_b, rights, partners, total
    )


def solution(mesh):
    placed = (
        P(None, "lsec", None, "rsec"),
        P(None, "lsec", "rsec", None),
        P(None, "rsec", "lsec", None),
        P("lsec"),
        P("rsec"),
        P(),
    )
    return jax.shard_map(
        local, mesh=mesh, in_specs=placed, out_specs=P(None, "lsec", None, "rsec"), check_vma=False
    )
```

```python
import functools

import jax
import jax.numpy as jnp
from jax import lax
from jax.experimental import pallas as pl
from jax.experimental.pallas import tpu as pltpu
from jax.sharding import PartitionSpec as P


KCH = 34
SHIFT = 2
SPLIT = 16
STAGED = 4
XN, ZN, YN, CORES = 4, 4, 4, 2
NT = (((1,), (1,)), ((), ()))
NN = (((1,), (0,)), ((), ()))


def shifted_x(step):
    return [(ZN * x + z, ZN * ((x + step) % XN) + z) for x in range(XN) for z in range(ZN)]


def shifted_z(step):
    return [(ZN * x + z, ZN * x + (z + step) % ZN) for x in range(XN) for z in range(ZN)]


def shifted_y(step):
    return [(CORES * y + c, CORES * ((y + step) % YN) + c) for y in range(YN) for c in range(CORES)]


def mask_kernel(left_size, right_size, two_site, down, up):
    row = lax.broadcasted_iota(jnp.int32, (128, 128), 0)
    col = lax.broadcasted_iota(jnp.int32, (128, 128), 1)
    for l in range(4):
        for r in range(4):
            live = (row < left_size[l]) & (col < right_size[r])
            target = down if r < 2 else up
            for v in range(2):
                block = two_site[v, l, :, r * 128 : r * 128 + 128].astype(jnp.float32)
                target[r % 2, l, v * 128 : v * 128 + 128] = jnp.where(live, block, 0.0).astype(
                    jnp.bfloat16
                )


def masked_halves(two_site, left_size, right_size):
    half = jax.ShapeDtypeStruct((2, 4, 256, 128), jnp.bfloat16)
    smem = pl.BlockSpec(memory_space=pltpu.SMEM)
    vmem = pl.BlockSpec(memory_space=pltpu.VMEM)
    return pl.pallas_call(
        mask_kernel,
        out_shape=(half, half),
        in_specs=[smem, smem, vmem],
        out_specs=(vmem, vmem),
        compiler_params=pltpu.CompilerParams(vmem_limit_bytes=8 << 20),
        cost_estimate=pl.CostEstimate(flops=1 << 20, bytes_accessed=2 << 20, transcendentals=0),
    )(left_size, right_size, two_site)


def rim_kernel(low_r, down, up, high_r, to_next, to_previous):
    for at, part in enumerate((low_r, down, up, high_r)):
        to_next[2 * at : 2 * at + 2] = part[:, 2:4]
        to_previous[2 * at : 2 * at + 2] = part[:, 0:2]


def left_rims(low_r, down, up, high_r):
    rim = jax.ShapeDtypeStruct((8, 2, 256, 128), jnp.bfloat16)
    vmem = pl.BlockSpec(memory_space=pltpu.VMEM)
    return pl.pallas_call(
        rim_kernel,
        out_shape=(rim, rim),
        in_specs=[vmem] * 4,
        out_specs=(vmem, vmem),
        compiler_params=pltpu.CompilerParams(vmem_limit_bytes=12 << 20),
        cost_estimate=pl.CostEstimate(flops=1 << 20, bytes_accessed=4 << 20, transcendentals=0),
    )(low_r, down, up, high_r)


def split_kernel(whole, first, second):
    first[...] = whole[:SPLIT]
    second[...] = whole[SPLIT:]


def split_channels(left_env):
    vmem = pl.BlockSpec(memory_space=pltpu.VMEM)
    return pl.pallas_call(
        split_kernel,
        out_shape=tuple(
            jax.ShapeDtypeStruct((many, 4, 8, 128), jnp.bfloat16) for many in (SPLIT, KCH - SPLIT)
        ),
        in_specs=[vmem],
        out_specs=(vmem, vmem),
        compiler_params=pltpu.CompilerParams(vmem_limit_bytes=8 << 20),
        cost_estimate=pl.CostEstimate(flops=1 << 20, bytes_accessed=1 << 20, transcendentals=0),
    )(left_env)


def bundle_kernel(own, left, right, far, out):
    for at, part in enumerate((own, left, right, far)):
        out[at] = part[...]


def bundled(own, left, right, far):
    vmem = pl.BlockSpec(memory_space=pltpu.VMEM)
    return pl.pallas_call(
        bundle_kernel,
        out_shape=jax.ShapeDtypeStruct((4, *own.shape), jnp.bfloat16),
        in_specs=[vmem] * 4,
        out_specs=vmem,
        compiler_params=pltpu.CompilerParams(vmem_limit_bytes=8 << 20),
        cost_estimate=pl.CostEstimate(flops=1 << 20, bytes_accessed=1 << 20, transcendentals=0),
    )(own, left, right, far)


RING_STEPS = (0, -1, 1, 2)


def channels_kernel(
    first, count, is_first, is_last, shift, left_size, right_size,
    low_r, down, up, high_r, low_l, high_l, lefts, rights, partners, *rest,
):
    rest = list(rest)
    total_in = None if is_first else rest.pop(0)
    out = rest.pop(0)
    source, left_all, right_all = rest[:3]
    rest = rest[3:]
    total, carried = (rest.pop(0), rest.pop(0)) if is_last else (out, None)
    sems = rest.pop(0)
    rsec, lsec = lax.axis_index("rsec"), lax.axis_index("lsec")
    x, z, y, core = rsec // ZN, lax.rem(rsec, ZN), lsec // CORES, lax.rem(lsec, CORES)

    waits = []

    def start(src, dst):
        copy = pltpu.make_async_copy(src, dst, sems.at[len(waits)])
        copy.start()
        waits.append(copy)

    for at, part in enumerate((low_r, down, up, high_r)):
        start(part, source.at[2 * at : 2 * at + 2, 2:6])
    start(low_l, source.at[:, 0:2])
    start(high_l, source.at[:, 6:8])
    ready = []
    for begin, end in ((0, STAGED), (STAGED, count)):
        for step, own, other in zip(RING_STEPS, rights, partners):
            for part, side in ((own, core), (other, 1 - core)):
                row = pl.multiple_of(16 * (CORES * lax.rem(y + step + YN, YN) + side), 16)
                start(
                    part.at[first + begin : first + end],
                    right_all.at[begin:end, :, pl.ds(row, 16)],
                )
        for outer, bundle in zip(RING_STEPS, lefts):
            for at, inner in enumerate(RING_STEPS):
                dx, dz = (outer, inner) if is_first else (inner, outer)
                row = 8 * (ZN * lax.rem(x + dx + XN, XN) + lax.rem(z + dz + ZN, ZN))
                start(
                    bundle.at[at, begin:end],
                    left_all.at[begin:end, :, pl.ds(pl.multiple_of(row, 8), 8)],
                )
        ready.append(len(waits))
    if not is_first:
        start(total_in, carried)
    total[...] = jnp.zeros_like(total)

    def add_channels(ks):
        shifts = [(shift[first + k, 0], shift[first + k, 1]) for k in ks]
        for r in range(4):
            partial = []
            for k, (dl, dr) in zip(ks, shifts):
                rows = source[r + SHIFT - dr, pl.ds(SHIFT - dl, 4)].reshape(4 * 256, 128)
                partial.append(
                    lax.dot_general(
                        rows, right_all[k, r], NT, preferred_element_type=jnp.float32
                    ).astype(jnp.bfloat16)
                )
            for l in range(4):
                added = None
                for at in range(0, len(ks), 2):
                    stacked = jnp.concatenate(
                        [
                            jnp.concatenate(
                                [p[l * 256 : l * 256 + 128], p[l * 256 + 128 : l * 256 + 256]],
                                axis=1,
                            )
                            for p in partial[at : at + 2]
                        ],
                        axis=0,
                    )
                    sides = jnp.concatenate([left_all[k, l] for k in ks[at : at + 2]], axis=1)
                    product = lax.dot_general(
                        sides, stacked, NN, preferred_element_type=jnp.float32
                    )
                    added = product if added is None else added + product
                total[l, r] += added

    def four_channels(group, carry):
        add_channels([4 * group + j for j in range(4)])
        return carry

    for copy in waits[: ready[0]]:
        copy.wait()
    add_channels(list(range(STAGED)))
    for copy in waits[ready[0] : ready[1]]:
        copy.wait()
    lax.fori_loop(1, count // 4, four_channels, 0)
    if count % 4:
        add_channels(list(range(count // 4 * 4, count)))
    for copy in waits[ready[1] :]:
        copy.wait()

    if is_last:
        row = lax.broadcasted_iota(jnp.int32, (128, 128), 0)
        col = lax.broadcasted_iota(jnp.int32, (128, 128), 1)
        for l in range(4):
            for r in range(4):
                live = (row < left_size[l]) & (col < right_size[r])
                for v in range(2):
                    lanes = slice(v * 128, v * 128 + 128)
                    block = total[l, r, :, lanes] + carried[l, r, :, lanes]
                    out[v, l, :, r * 128 : r * 128 + 128] = jnp.where(live, block, 0.0).astype(
                        jnp.bfloat16
                    )


def run_channels(first, count, is_first, is_last, scalars, sources, lefts, rights, partners, total):
    totals = jax.ShapeDtypeStruct((4, 4, 128, 256), jnp.float32)
    result = jax.ShapeDtypeStruct((2, 4, 128, 512), jnp.bfloat16)
    anywhere = pl.BlockSpec(memory_space=pltpu.HBM)
    smem = pl.BlockSpec(memory_space=pltpu.SMEM)
    operands = [*scalars, *sources, tuple(lefts), tuple(rights), tuple(partners)]
    specs = [smem] * 3 + [anywhere] * 6 + [(anywhere,) * 4] * 3
    if not is_first:
        operands.append(total)
        specs.append(anywhere)
    scratch = [
        pltpu.VMEM((8, 8, 256, 128), jnp.bfloat16),
        pltpu.VMEM((count, 4, 128, 128), jnp.bfloat16),
        pltpu.VMEM((count, 4, 128, 128), jnp.bfloat16),
    ]
    if is_last:
        scratch += [pltpu.VMEM((4, 4, 128, 256), jnp.float32)] * 2
    scratch.append(pltpu.SemaphoreType.DMA((56,)))
    return pl.pallas_call(
        functools.partial(channels_kernel, first, count, is_first, is_last),
        out_shape=result if is_last else totals,
        in_specs=specs,
        out_specs=pl.BlockSpec(memory_space=pltpu.VMEM),
        scratch_shapes=scratch,
        compiler_params=pltpu.CompilerParams(vmem_limit_bytes=60 * 1024 * 1024),
        cost_estimate=pl.CostEstimate(
            flops=count * 4 * 4 * 2 * 2 * 2 * 128**3, bytes_accessed=10 << 20, transcendentals=0
        ),
    )(*operands)


def applied(two_site, left_env, right_env, left_size, right_size, channel_shift):
    steps = (1, -1, 2)
    rights = [right_env] + [lax.ppermute(right_env, "lsec", shifted_y(steps[i])) for i in range(3)]
    part_a, part_b = split_channels(left_env)
    ring_a = [lax.ppermute(part_a, "rsec", shifted_z(steps[i])) for i in range(3)]
    ring_b = [lax.ppermute(part_b, "rsec", shifted_x(steps[i])) for i in range(3)]

    down, up = masked_halves(two_site, left_size, right_size)
    l_up = [(i, i + 1) for i in range(7)]
    l_down = [(i + 1, i) for i in range(7)]
    r_up = [(i, i + 1) for i in range(15)]
    r_down = [(i + 1, i) for i in range(15)]
    low_r = lax.ppermute(up, "rsec", r_up)
    high_r = lax.ppermute(down, "rsec", r_down)

    bundle_a = bundled(part_a, *ring_a)
    lefts_a = [bundle_a] + [lax.ppermute(bundle_a, "rsec", shifted_x(steps[i])) for i in range(3)]
    to_next, to_previous = left_rims(low_r, down, up, high_r)
    low_l = lax.ppermute(to_next, "lsec", l_up)
    high_l = lax.ppermute(to_previous, "lsec", l_down)

    swap = [(i, i ^ 1) for i in range(8)]
    partners = [lax.ppermute(part, "lsec", swap) for part in rights]

    bundle_b = bundled(part_b, *ring_b)
    lefts_b = [bundle_b] + [lax.ppermute(bundle_b, "rsec", shifted_z(steps[i])) for i in range(3)]

    scalars = (channel_shift, left_size, right_size)
    sources = (low_r, down, up, high_r, low_l, high_l)
    total = run_channels(0, SPLIT, True, False, scalars, sources, lefts_a, rights, partners, None)
    return run_channels(
        SPLIT, KCH - SPLIT, False, True, scalars, sources, lefts_b, rights, partners, total,
    )


def solution(mesh):
    placed = (
        P(None, "lsec", None, "rsec"),
        P(None, "lsec", "rsec", None),
        P(None, "rsec", "lsec", None),
        P("lsec"),
        P("rsec"),
        P(),
    )
    return jax.shard_map(
        applied, mesh=mesh, in_specs=placed, out_specs=P(None, "lsec", None, "rsec"), check_vma=False
    )
```

```python
import functools

import jax
import jax.numpy as jnp
from jax import lax
from jax.experimental import pallas as pl
from jax.experimental.pallas import tpu as pltpu
from jax.sharding import PartitionSpec as P


KCH = 34
SHIFT = 2
SPLIT = 16
STAGED = 4
XN, ZN, YN, CORES = 4, 4, 4, 2
NT = (((1,), (1,)), ((), ()))
NN = (((1,), (0,)), ((), ()))


def shifted_x(step):
    return [(ZN * x + z, ZN * ((x + step) % XN) + z) for x in range(XN) for z in range(ZN)]


def shifted_z(step):
    return [(ZN * x + z, ZN * x + (z + step) % ZN) for x in range(XN) for z in range(ZN)]


def shifted_y(step):
    return [(CORES * y + c, CORES * ((y + step) % YN) + c) for y in range(YN) for c in range(CORES)]


def prepare_kernel(
    left_size, right_size, two_site, left_env, first, second, down, up,
    rows_live, cols_live, held, env, sems,
):
    pairs = ((left_env, env), (left_size, rows_live), (right_size, cols_live), (two_site, held))
    copies = [
        pltpu.make_async_copy(src, dst, sems.at[at]) for at, (src, dst) in enumerate(pairs)
    ]
    for copy in copies:
        copy.start()
    copies[0].wait()
    first[...] = env[:SPLIT]
    second[...] = env[SPLIT:]
    for copy in copies[1:]:
        copy.wait()
    row = lax.broadcasted_iota(jnp.int32, (128, 128), 0)
    col = lax.broadcasted_iota(jnp.int32, (128, 128), 1)
    for l in range(4):
        for r in range(4):
            live = (row < rows_live[l]) & (col < cols_live[r])
            target = down if r < 2 else up
            for v in range(2):
                block = held[v, l, :, r * 128 : r * 128 + 128].astype(jnp.float32)
                target[r % 2, l, v * 128 : v * 128 + 128] = jnp.where(live, block, 0.0).astype(
                    jnp.bfloat16
                )


def prepared(two_site, left_env, left_size, right_size):
    half = jax.ShapeDtypeStruct((2, 4, 256, 128), jnp.bfloat16)
    parts = [
        jax.ShapeDtypeStruct((many, 4, 8, 128), jnp.bfloat16) for many in (SPLIT, KCH - SPLIT)
    ]
    return pl.pallas_call(
        prepare_kernel,
        out_shape=(*parts, half, half),
        in_specs=[pl.BlockSpec(memory_space=pltpu.HBM)] * 4,
        out_specs=(pl.BlockSpec(memory_space=pltpu.VMEM),) * 4,
        scratch_shapes=[
            pltpu.SMEM((4,), jnp.int32),
            pltpu.SMEM((4,), jnp.int32),
            pltpu.VMEM(two_site.shape, jnp.bfloat16),
            pltpu.VMEM(left_env.shape, jnp.bfloat16),
            pltpu.SemaphoreType.DMA((4,)),
        ],
        compiler_params=pltpu.CompilerParams(vmem_limit_bytes=60 * 1024 * 1024),
        cost_estimate=pl.CostEstimate(flops=1 << 20, bytes_accessed=2 << 20, transcendentals=0),
    )(left_size, right_size, two_site, left_env)


def rim_kernel(low_r, down, up, high_r, to_next, to_previous):
    for at, part in enumerate((low_r, down, up, high_r)):
        to_next[2 * at : 2 * at + 2] = part[:, 2:4]
        to_previous[2 * at : 2 * at + 2] = part[:, 0:2]


def left_rims(low_r, down, up, high_r):
    rim = jax.ShapeDtypeStruct((8, 2, 256, 128), jnp.bfloat16)
    vmem = pl.BlockSpec(memory_space=pltpu.VMEM)
    return pl.pallas_call(
        rim_kernel,
        out_shape=(rim, rim),
        in_specs=[vmem] * 4,
        out_specs=(vmem, vmem),
        compiler_params=pltpu.CompilerParams(vmem_limit_bytes=12 << 20),
        cost_estimate=pl.CostEstimate(flops=1 << 20, bytes_accessed=4 << 20, transcendentals=0),
    )(low_r, down, up, high_r)


def bundle_kernel(own, left, right, far, out):
    for at, part in enumerate((own, left, right, far)):
        out[at] = part[...]


def bundled(own, left, right, far):
    vmem = pl.BlockSpec(memory_space=pltpu.VMEM)
    return pl.pallas_call(
        bundle_kernel,
        out_shape=jax.ShapeDtypeStruct((4, *own.shape), jnp.bfloat16),
        in_specs=[vmem] * 4,
        out_specs=vmem,
        compiler_params=pltpu.CompilerParams(vmem_limit_bytes=8 << 20),
        cost_estimate=pl.CostEstimate(flops=1 << 20, bytes_accessed=1 << 20, transcendentals=0),
    )(own, left, right, far)


RING_STEPS = (0, -1, 1, 2)


def channels_kernel(
    first, count, is_first, is_last, shift, left_size, right_size,
    low_r, down, up, high_r, low_l, high_l, lefts, rights, partners, *rest,
):
    rest = list(rest)
    total_in = None if is_first else rest.pop(0)
    out = rest.pop(0)
    source, left_all, right_all = rest[:3]
    rest = rest[3:]
    total, carried = (rest.pop(0), rest.pop(0)) if is_last else (out, None)
    sems = rest.pop(0)
    rsec, lsec = lax.axis_index("rsec"), lax.axis_index("lsec")
    x, z, y, core = rsec // ZN, lax.rem(rsec, ZN), lsec // CORES, lax.rem(lsec, CORES)

    waits = []

    def start(src, dst):
        copy = pltpu.make_async_copy(src, dst, sems.at[len(waits)])
        copy.start()
        waits.append(copy)

    for at, part in enumerate((low_r, down, up, high_r)):
        start(part, source.at[2 * at : 2 * at + 2, 2:6])
    start(low_l, source.at[:, 0:2])
    start(high_l, source.at[:, 6:8])
    ready = []
    for begin, end in ((0, STAGED), (STAGED, count)):
        for step, own, other in zip(RING_STEPS, rights, partners):
            for part, side in ((own, core), (other, 1 - core)):
                row = pl.multiple_of(16 * (CORES * lax.rem(y + step + YN, YN) + side), 16)
                start(
                    part.at[first + begin : first + end],
                    right_all.at[begin:end, :, pl.ds(row, 16)],
                )
        for outer, bundle in zip(RING_STEPS, lefts):
            for at, inner in enumerate(RING_STEPS):
                dx, dz = (outer, inner) if is_first else (inner, outer)
                row = 8 * (ZN * lax.rem(x + dx + XN, XN) + lax.rem(z + dz + ZN, ZN))
                start(
                    bundle.at[at, begin:end],
                    left_all.at[begin:end, :, pl.ds(pl.multiple_of(row, 8), 8)],
                )
        ready.append(len(waits))
    if not is_first:
        start(total_in, carried)

    def add_channels(ks, fresh=False):
        shifts = [(shift[0, first + k], shift[1, first + k]) for k in ks]
        for r in range(4):
            partial = []
            for k, (dl, dr) in zip(ks, shifts):
                rows = source[r + SHIFT - dr, pl.ds(SHIFT - dl, 4)].reshape(4 * 256, 128)
                partial.append(
                    lax.dot_general(
                        rows, right_all[k, r], NT, preferred_element_type=jnp.float32
                    ).astype(jnp.bfloat16)
                )
            for l in range(4):
                added = None
                for at in range(0, len(ks), 2):
                    stacked = jnp.concatenate(
                        [
                            jnp.concatenate(
                                [p[l * 256 : l * 256 + 128], p[l * 256 + 128 : l * 256 + 256]],
                                axis=1,
                            )
                            for p in partial[at : at + 2]
                        ],
                        axis=0,
                    )
                    sides = jnp.concatenate([left_all[k, l] for k in ks[at : at + 2]], axis=1)
                    product = lax.dot_general(
                        sides, stacked, NN, preferred_element_type=jnp.float32
                    )
                    added = product if added is None else added + product
                total[l, r] = added if fresh else total[l, r] + added

    def four_channels(group, carry):
        add_channels([4 * group + j for j in range(4)])
        return carry

    for copy in waits[: ready[0]]:
        copy.wait()
    add_channels(list(range(STAGED)), fresh=True)
    for copy in waits[ready[0] : ready[1]]:
        copy.wait()
    lax.fori_loop(1, count // 4, four_channels, 0)
    if count % 4:
        add_channels(list(range(count // 4 * 4, count)))
    for copy in waits[ready[1] :]:
        copy.wait()

    if is_last:
        row = lax.broadcasted_iota(jnp.int32, (128, 128), 0)
        col = lax.broadcasted_iota(jnp.int32, (128, 128), 1)
        for l in range(4):
            for r in range(4):
                live = (row < left_size[l]) & (col < right_size[r])
                for v in range(2):
                    lanes = slice(v * 128, v * 128 + 128)
                    block = total[l, r, :, lanes] + carried[l, r, :, lanes]
                    out[v, l, :, r * 128 : r * 128 + 128] = jnp.where(live, block, 0.0).astype(
                        jnp.bfloat16
                    )


def run_channels(first, count, is_first, is_last, scalars, sources, lefts, rights, partners, total):
    totals = jax.ShapeDtypeStruct((4, 4, 128, 256), jnp.float32)
    result = jax.ShapeDtypeStruct((2, 4, 128, 512), jnp.bfloat16)
    anywhere = pl.BlockSpec(memory_space=pltpu.HBM)
    smem = pl.BlockSpec(memory_space=pltpu.SMEM)
    operands = [*scalars, *sources, tuple(lefts), tuple(rights), tuple(partners)]
    specs = [smem] * 3 + [anywhere] * 6 + [(anywhere,) * 4] * 3
    if not is_first:
        operands.append(total)
        specs.append(anywhere)
    scratch = [
        pltpu.VMEM((8, 8, 256, 128), jnp.bfloat16),
        pltpu.VMEM((count, 4, 128, 128), jnp.bfloat16),
        pltpu.VMEM((count, 4, 128, 128), jnp.bfloat16),
    ]
    if is_last:
        scratch += [pltpu.VMEM((4, 4, 128, 256), jnp.float32)] * 2
    scratch.append(pltpu.SemaphoreType.DMA((56,)))
    return pl.pallas_call(
        functools.partial(channels_kernel, first, count, is_first, is_last),
        out_shape=result if is_last else totals,
        in_specs=specs,
        out_specs=pl.BlockSpec(memory_space=pltpu.VMEM),
        scratch_shapes=scratch,
        compiler_params=pltpu.CompilerParams(vmem_limit_bytes=60 * 1024 * 1024),
        cost_estimate=pl.CostEstimate(
            flops=count * 4 * 4 * 2 * 2 * 2 * 128**3, bytes_accessed=10 << 20, transcendentals=0
        ),
    )(*operands)


def applied(two_site, left_env, right_env, left_size, right_size, channel_shift):
    steps = (1, -1, 2)
    rights = [right_env] + [lax.ppermute(right_env, "lsec", shifted_y(steps[i])) for i in range(3)]
    part_a, part_b, down, up = prepared(two_site, left_env, left_size, right_size)
    ring_a = [lax.ppermute(part_a, "rsec", shifted_z(steps[i])) for i in range(3)]
    ring_b = [lax.ppermute(part_b, "rsec", shifted_x(steps[i])) for i in range(3)]

    l_up = [(i, i + 1) for i in range(7)]
    l_down = [(i + 1, i) for i in range(7)]
    r_up = [(i, i + 1) for i in range(15)]
    r_down = [(i + 1, i) for i in range(15)]
    low_r = lax.ppermute(up, "rsec", r_up)
    high_r = lax.ppermute(down, "rsec", r_down)

    bundle_a = bundled(part_a, *ring_a)
    lefts_a = [bundle_a] + [lax.ppermute(bundle_a, "rsec", shifted_x(steps[i])) for i in range(3)]
    to_next, to_previous = left_rims(low_r, down, up, high_r)
    low_l = lax.ppermute(to_next, "lsec", l_up)
    high_l = lax.ppermute(to_previous, "lsec", l_down)

    swap = [(i, i ^ 1) for i in range(8)]
    partners = [lax.ppermute(part, "lsec", swap) for part in rights]

    bundle_b = bundled(part_b, *ring_b)
    lefts_b = [bundle_b] + [lax.ppermute(bundle_b, "rsec", shifted_z(steps[i])) for i in range(3)]

    scalars = (channel_shift.T, left_size, right_size)
    sources = (low_r, down, up, high_r, low_l, high_l)
    total = run_channels(0, SPLIT, True, False, scalars, sources, lefts_a, rights, partners, None)
    return run_channels(
        SPLIT, KCH - SPLIT, False, True, scalars, sources, lefts_b, rights, partners, total,
    )


def solution(mesh):
    placed = (
        P(None, "lsec", None, "rsec"),
        P(None, "lsec", "rsec", None),
        P(None, "rsec", "lsec", None),
        P("lsec"),
        P("rsec"),
        P(),
    )
    return jax.shard_map(
        applied, mesh=mesh, in_specs=placed, out_specs=P(None, "lsec", None, "rsec"), check_vma=False
    )
```

```python
import functools

import jax
import jax.numpy as jnp
from jax import lax
from jax.experimental import pallas as pl
from jax.experimental.pallas import tpu as pltpu
from jax.sharding import PartitionSpec as P


KCH = 34
SHIFT = 2
SPLIT = 16
STAGED = 4
XN, ZN, YN, CORES = 4, 4, 4, 2
NT = (((1,), (1,)), ((), ()))
NN = (((1,), (0,)), ((), ()))


def shifted_x(step):
    return [(ZN * x + z, ZN * ((x + step) % XN) + z) for x in range(XN) for z in range(ZN)]


def shifted_z(step):
    return [(ZN * x + z, ZN * x + (z + step) % ZN) for x in range(XN) for z in range(ZN)]


def shifted_y(step):
    return [(CORES * y + c, CORES * ((y + step) % YN) + c) for y in range(YN) for c in range(CORES)]


def prepare_kernel(
    left_size, right_size, two_site, left_env, first, second, down, up,
    rows_live, cols_live, held, env, sems,
):
    pairs = ((left_env, env), (left_size, rows_live), (right_size, cols_live), (two_site, held))
    copies = [
        pltpu.make_async_copy(src, dst, sems.at[at]) for at, (src, dst) in enumerate(pairs)
    ]
    for copy in copies:
        copy.start()
    copies[0].wait()
    first[...] = env[:SPLIT]
    second[...] = env[SPLIT:]
    for copy in copies[1:]:
        copy.wait()
    row = lax.broadcasted_iota(jnp.int32, (128, 128), 0)
    col = lax.broadcasted_iota(jnp.int32, (128, 128), 1)
    for l in range(4):
        for r in range(4):
            live = (row < rows_live[l]) & (col < cols_live[r])
            target = down if r < 2 else up
            for v in range(2):
                block = held[v, l, :, r * 128 : r * 128 + 128].astype(jnp.float32)
                target[r % 2, l, v * 128 : v * 128 + 128] = jnp.where(live, block, 0.0).astype(
                    jnp.bfloat16
                )


def prepared(two_site, left_env, left_size, right_size):
    half = jax.ShapeDtypeStruct((2, 4, 256, 128), jnp.bfloat16)
    parts = [
        jax.ShapeDtypeStruct((many, 4, 8, 128), jnp.bfloat16) for many in (SPLIT, KCH - SPLIT)
    ]
    return pl.pallas_call(
        prepare_kernel,
        out_shape=(*parts, half, half),
        in_specs=[pl.BlockSpec(memory_space=pltpu.HBM)] * 4,
        out_specs=(pl.BlockSpec(memory_space=pltpu.VMEM),) * 4,
        scratch_shapes=[
            pltpu.SMEM((4,), jnp.int32),
            pltpu.SMEM((4,), jnp.int32),
            pltpu.VMEM(two_site.shape, jnp.bfloat16),
            pltpu.VMEM(left_env.shape, jnp.bfloat16),
            pltpu.SemaphoreType.DMA((4,)),
        ],
        compiler_params=pltpu.CompilerParams(vmem_limit_bytes=60 * 1024 * 1024),
        cost_estimate=pl.CostEstimate(flops=1 << 20, bytes_accessed=2 << 20, transcendentals=0),
    )(left_size, right_size, two_site, left_env)


def rim_kernel(low_r, down, up, high_r, to_next, to_previous):
    for at, part in enumerate((low_r, down, up, high_r)):
        to_next[2 * at : 2 * at + 2] = part[:, 2:4]
        to_previous[2 * at : 2 * at + 2] = part[:, 0:2]


def left_rims(low_r, down, up, high_r):
    rim = jax.ShapeDtypeStruct((8, 2, 256, 128), jnp.bfloat16)
    vmem = pl.BlockSpec(memory_space=pltpu.VMEM)
    return pl.pallas_call(
        rim_kernel,
        out_shape=(rim, rim),
        in_specs=[vmem] * 4,
        out_specs=(vmem, vmem),
        compiler_params=pltpu.CompilerParams(vmem_limit_bytes=12 << 20),
        cost_estimate=pl.CostEstimate(flops=1 << 20, bytes_accessed=4 << 20, transcendentals=0),
    )(low_r, down, up, high_r)


def bundle_kernel(own, left, right, far, out):
    for at, part in enumerate((own, left, right, far)):
        out[at] = part[...]


def bundled(own, left, right, far):
    vmem = pl.BlockSpec(memory_space=pltpu.VMEM)
    return pl.pallas_call(
        bundle_kernel,
        out_shape=jax.ShapeDtypeStruct((4, *own.shape), jnp.bfloat16),
        in_specs=[vmem] * 4,
        out_specs=vmem,
        compiler_params=pltpu.CompilerParams(vmem_limit_bytes=8 << 20),
        cost_estimate=pl.CostEstimate(flops=1 << 20, bytes_accessed=1 << 20, transcendentals=0),
    )(own, left, right, far)


RING_STEPS = (0, -1, 1, 2)


def channels_kernel(
    first, count, is_first, is_last, shift, left_size, right_size,
    low_r, down, up, high_r, low_l, high_l, lefts, rights, partners, *rest,
):
    rest = list(rest)
    total_in = None if is_first else rest.pop(0)
    out = rest.pop(0)
    source, left_all, right_all = rest[:3]
    rest = rest[3:]
    total = rest.pop(0)
    carried = rest.pop(0) if is_last else None
    sems = rest.pop(0)
    rsec, lsec = lax.axis_index("rsec"), lax.axis_index("lsec")
    x, z, y, core = rsec // ZN, lax.rem(rsec, ZN), lsec // CORES, lax.rem(lsec, CORES)

    waits = []

    def start(src, dst):
        copy = pltpu.make_async_copy(src, dst, sems.at[len(waits)])
        copy.start()
        waits.append(copy)

    for at, part in enumerate((low_r, down, up, high_r)):
        start(part, source.at[2 * at : 2 * at + 2, 2:6])
    start(low_l, source.at[:, 0:2])
    start(high_l, source.at[:, 6:8])
    ready = []
    for begin, end in ((0, STAGED), (STAGED, count)):
        for step, own, other in zip(RING_STEPS, rights, partners):
            for part, side in ((own, core), (other, 1 - core)):
                row = pl.multiple_of(16 * (CORES * lax.rem(y + step + YN, YN) + side), 16)
                start(
                    part.at[first + begin : first + end],
                    right_all.at[begin:end, :, pl.ds(row, 16)],
                )
        for outer, bundle in zip(RING_STEPS, lefts):
            for at, inner in enumerate(RING_STEPS):
                dx, dz = (outer, inner) if is_first else (inner, outer)
                row = 8 * (ZN * lax.rem(x + dx + XN, XN) + lax.rem(z + dz + ZN, ZN))
                start(
                    bundle.at[at, begin:end],
                    left_all.at[begin:end, :, pl.ds(pl.multiple_of(row, 8), 8)],
                )
        ready.append(len(waits))
    if not is_first:
        start(total_in, carried)

    def add_channels(ks, fresh=False, finish=None, after_column=None):
        shifts = [(shift[0, first + k], shift[1, first + k]) for k in ks]
        for r in range(4):
            partial = []
            for k, (dl, dr) in zip(ks, shifts):
                rows = source[r + SHIFT - dr, pl.ds(SHIFT - dl, 4)].reshape(4 * 256, 128)
                partial.append(
                    lax.dot_general(
                        rows, right_all[k, r], NT, preferred_element_type=jnp.float32
                    ).astype(jnp.bfloat16)
                )
            for l in range(4):
                added = None
                for at in range(0, len(ks), 2):
                    stacked = jnp.concatenate(
                        [
                            jnp.concatenate(
                                [p[l * 256 : l * 256 + 128], p[l * 256 + 128 : l * 256 + 256]],
                                axis=1,
                            )
                            for p in partial[at : at + 2]
                        ],
                        axis=0,
                    )
                    sides = jnp.concatenate([left_all[k, l] for k in ks[at : at + 2]], axis=1)
                    product = lax.dot_general(
                        sides, stacked, NN, preferred_element_type=jnp.float32
                    )
                    added = product if added is None else added + product
                value = added if fresh else total[l, r] + added
                if finish is None:
                    total[l, r] = value
                else:
                    finish(l, r, value)
            if after_column is not None:
                after_column(r)

    def four_channels(group, carry):
        add_channels([4 * group + j for j in range(4)])
        return carry

    for copy in waits[: ready[0]]:
        copy.wait()
    add_channels(list(range(STAGED)), fresh=True)
    for copy in waits[ready[0] : ready[1]]:
        copy.wait()
    final = count // 4 * 4 if count % 4 else count - 4
    lax.fori_loop(1, final // 4, four_channels, 0)
    last_ks = list(range(final, count))
    for copy in waits[ready[1] :]:
        copy.wait()

    if not is_last:
        flushes = [
            pltpu.make_async_copy(total.at[:, r], out.at[:, r], sems.at[r]) for r in range(4)
        ]

        def after_column(r):
            if r > 0:
                flushes[r - 1].start()

        add_channels(last_ks, after_column=after_column)
        flushes[3].start()
        for copy in flushes:
            copy.wait()
        return

    row = lax.broadcasted_iota(jnp.int32, (128, 128), 0)
    col = lax.broadcasted_iota(jnp.int32, (128, 128), 1)

    def finish(l, r, value):
        live = (row < left_size[l]) & (col < right_size[r])
        for v in range(2):
            lanes = slice(v * 128, v * 128 + 128)
            block = value[:, lanes] + carried[l, r, :, lanes]
            out[v, l, :, r * 128 : r * 128 + 128] = jnp.where(live, block, 0.0).astype(jnp.bfloat16)

    add_channels(last_ks, finish=finish)


def run_channels(first, count, is_first, is_last, scalars, sources, lefts, rights, partners, total):
    totals = jax.ShapeDtypeStruct((4, 4, 128, 256), jnp.float32)
    result = jax.ShapeDtypeStruct((2, 4, 128, 512), jnp.bfloat16)
    anywhere = pl.BlockSpec(memory_space=pltpu.HBM)
    smem = pl.BlockSpec(memory_space=pltpu.SMEM)
    operands = [*scalars, *sources, tuple(lefts), tuple(rights), tuple(partners)]
    specs = [smem] * 3 + [anywhere] * 6 + [(anywhere,) * 4] * 3
    if not is_first:
        operands.append(total)
        specs.append(anywhere)
    scratch = [
        pltpu.VMEM((8, 8, 256, 128), jnp.bfloat16),
        pltpu.VMEM((count, 4, 128, 128), jnp.bfloat16),
        pltpu.VMEM((count, 4, 128, 128), jnp.bfloat16),
    ]
    scratch += [pltpu.VMEM((4, 4, 128, 256), jnp.float32)] * (2 if is_last else 1)
    scratch.append(pltpu.SemaphoreType.DMA((56,)))
    return pl.pallas_call(
        functools.partial(channels_kernel, first, count, is_first, is_last),
        out_shape=result if is_last else totals,
        in_specs=specs,
        out_specs=pl.BlockSpec(memory_space=pltpu.VMEM) if is_last else anywhere,
        scratch_shapes=scratch,
        compiler_params=pltpu.CompilerParams(vmem_limit_bytes=60 * 1024 * 1024),
        cost_estimate=pl.CostEstimate(
            flops=count * 4 * 4 * 2 * 2 * 2 * 128**3, bytes_accessed=10 << 20, transcendentals=0
        ),
    )(*operands)


def applied(two_site, left_env, right_env, left_size, right_size, channel_shift):
    steps = (1, -1, 2)
    rights = [right_env] + [lax.ppermute(right_env, "lsec", shifted_y(steps[i])) for i in range(3)]
    part_a, part_b, down, up = prepared(two_site, left_env, left_size, right_size)
    ring_a = [lax.ppermute(part_a, "rsec", shifted_z(steps[i])) for i in range(3)]
    ring_b = [lax.ppermute(part_b, "rsec", shifted_x(steps[i])) for i in range(3)]

    l_up = [(i, i + 1) for i in range(7)]
    l_down = [(i + 1, i) for i in range(7)]
    r_up = [(i, i + 1) for i in range(15)]
    r_down = [(i + 1, i) for i in range(15)]
    low_r = lax.ppermute(up, "rsec", r_up)
    high_r = lax.ppermute(down, "rsec", r_down)

    bundle_a = bundled(part_a, *ring_a)
    lefts_a = [bundle_a] + [lax.ppermute(bundle_a, "rsec", shifted_x(steps[i])) for i in range(3)]
    to_next, to_previous = left_rims(low_r, down, up, high_r)
    low_l = lax.ppermute(to_next, "lsec", l_up)
    high_l = lax.ppermute(to_previous, "lsec", l_down)

    swap = [(i, i ^ 1) for i in range(8)]
    partners = [lax.ppermute(part, "lsec", swap) for part in rights]

    bundle_b = bundled(part_b, *ring_b)
    lefts_b = [bundle_b] + [lax.ppermute(bundle_b, "rsec", shifted_z(steps[i])) for i in range(3)]

    scalars = (channel_shift.T, left_size, right_size)
    sources = (low_r, down, up, high_r, low_l, high_l)
    total = run_channels(0, SPLIT, True, False, scalars, sources, lefts_a, rights, partners, None)
    return run_channels(
        SPLIT, KCH - SPLIT, False, True, scalars, sources, lefts_b, rights, partners, total,
    )


def solution(mesh):
    placed = (
        P(None, "lsec", None, "rsec"),
        P(None, "lsec", "rsec", None),
        P(None, "rsec", "lsec", None),
        P("lsec"),
        P("rsec"),
        P(),
    )
    return jax.shard_map(
        applied, mesh=mesh, in_specs=placed, out_specs=P(None, "lsec", None, "rsec"), check_vma=False
    )
```
